32 devices in a mesh: grp: 4 (over y, x), mem: 8 (over z, core).
Axes of the slice: x: 2, y: 2, z: 4, core: 2. Of those that a mesh axis runs over, the one named last changes fastest.
Arguments:
- background_tensor: bfloat16 [64, 256, 1024], P('grp', 'mem'), may hold values from -6 to 6
- reading_tally: int32 [64], P(('grp', 'mem')), may hold values from 128 to 1024, as said below
- measurement_slot: int32 [64, 1024], P(('grp', 'mem')), may hold values from 0 to 1023
- reading_datum: float32 [64, 1024], P(('grp', 'mem')), may hold values from -6 to 6
- error_precision: float32 [64, 1024], P(('grp', 'mem')), may hold values from 0.5 to 16
- reading_offset: float32 [64, 1024], P(('grp', 'mem')), may hold values from 0 to 1
Outputs:
- analysis: bfloat16 [64, 256, 1024], P('grp', 'mem')
The draws below stay inside these ranges and needn't reach their ends.
Inputs may be any that keep to these rules, and one draw needn't show every extreme that they name: `reading_tally`: each column's live observations fill its first slots; at least one column has exactly 1024.
All inputs are finite; a program needn't handle non-finite values.
Results may differ from the reference program's by a relative error of at most 0.0074.
Values may be sent and summed in bfloat16 or wider, within the bound.
A program may use at most 64 MiB of HBM per device.

```python
import math
import jax
import jax.numpy as jnp
from jax import lax

MEMBER_NUMBER = 256
COLUMN_SIZE_VERT = 1024
MAXOBS = 1024
NSTEPS = 5
DOMAIN_SITES = 64


def draw_reading_tally(key, part):
    first, second, third = jax.random.split(jax.random.fold_in(key, 17), 3)
    level = jax.random.randint(first, (DOMAIN_SITES,), 0, 3)
    base = jnp.left_shift(jnp.full((DOMAIN_SITES,), MAXOBS // 8, jnp.int32), level)
    extra = jax.random.randint(second, (DOMAIN_SITES,), 0, 1048576) % base
    chosen = jax.random.randint(third, (), 0, DOMAIN_SITES)
    counts = jnp.where(jnp.arange(DOMAIN_SITES, dtype=jnp.int32) == chosen, MAXOBS, base + extra)
    return counts.astype(jnp.int32)


def set_ends(values, own_key, smallest, largest):
    longest = values.shape.index(max(values.shape))
    spots = []
    for shift in (0, 1):
        where = [jax.random.randint(jax.random.fold_in(own_key, axis), (), 0, length) for axis, length in enumerate(values.shape)]
        where[longest] = (where[longest] + shift) % values.shape[longest]
        spots.append(tuple(where))
    return values.at[spots[0]].set(smallest).at[spots[1]].set(largest)


def levels(own_key, shape, pieces, smallest, high):
    gain = 1.0
    for position, shards_of in pieces:
        draws = jax.random.uniform(jax.random.fold_in(jax.random.fold_in(own_key, 6), position), (shards_of,), jnp.float32, smallest / len(pieces), high / len(pieces))
        gain = gain * jnp.repeat(jnp.exp(draws), shape[position] // shards_of).reshape((-1,) + (1,) * (len(shape) - 1 - position))
    return gain


def scatter_about(rng, dims, width, reach, cuts=(), kind=jnp.bfloat16):
    values = width * jax.random.normal(rng, dims, jnp.float32)
    if cuts:
        values = values * levels(rng, dims, cuts, -0.22, 0.18)
    return jnp.clip(values, -reach, reach).astype(kind)


def setup_inputs(seed: int = 0) -> dict:
    splits = jax.random.split(jax.random.key(seed), 7)
    background_tensor = scatter_about(splits[0], (DOMAIN_SITES, MEMBER_NUMBER, COLUMN_SIZE_VERT), 1.0, 6.0, ((0, 4), (1, 8)))
    reading_tally = draw_reading_tally(jax.random.fold_in(splits[6], 71), 0)
    measurement_slot = set_ends(jax.random.randint(splits[2], (DOMAIN_SITES, MAXOBS), 0, COLUMN_SIZE_VERT), jax.random.fold_in(splits[2], 1), 0, COLUMN_SIZE_VERT - 1).astype(jnp.int32)
    reading_datum = scatter_about(splits[3], (DOMAIN_SITES, MAXOBS), 1.0, 6.0, ((0, 32),), jnp.float32)
    error_precision = jnp.clip(jnp.exp(math.log(16.0) - 3.465736 * jax.random.uniform(splits[4], (DOMAIN_SITES, MAXOBS), jnp.float32) ** levels(splits[4], (DOMAIN_SITES, MAXOBS), ((0, 32),), -0.2, 0.2)), 0.5, 16.0)
    reading_offset = jnp.clip(1.0 * jax.random.uniform(splits[5], (DOMAIN_SITES, MAXOBS), jnp.float32) ** levels(splits[5], (DOMAIN_SITES, MAXOBS), ((0, 32),), -0.2, 0.2), 0.0, 1.0)
    return dict(background_tensor=background_tensor, reading_tally=reading_tally, measurement_slot=measurement_slot, reading_datum=reading_datum, error_precision=error_precision, reading_offset=reading_offset)


def direction_weights(shift_amount):
    toward_west = jnp.exp(-(shift_amount + 0.5) ** 2)
    own_weight = jnp.exp(-(shift_amount - 0.5) ** 2)
    toward_east = jnp.exp(-(1.5 - shift_amount) ** 2)
    return (toward_west, own_weight, toward_east)

def local_summary(background_members):
    sample_slices = background_members.shape[0]
    model_vector32 = background_members.astype(jnp.float32)
    focal_site = lax.optimization_barrier(jnp.sum(model_vector32, axis=0)) / sample_slices
    anomaly_matrix = (model_vector32 - focal_site[None, :]).astype(jnp.bfloat16)
    return (focal_site, anomaly_matrix)

def local_measurements(background_members, position_number, quantity, scalar_amount, noise_weighting, shift_amount, lateral_neighbor):
    focal_site, anomaly_matrix = local_summary(background_members)
    obs_slots = position_number.shape[0]
    measured_vector = jnp.take(anomaly_matrix, position_number, axis=1)
    innovation = scalar_amount - jnp.take(focal_site, position_number, axis=0)
    live_mask = (jnp.arange(obs_slots, dtype=jnp.int32) < quantity).astype(jnp.float32)
    weight = direction_weights(shift_amount)[lateral_neighbor]
    factor = jnp.sqrt(weight * noise_weighting) * live_mask
    scaled = (measured_vector.astype(jnp.float32) * factor[None, :]).astype(jnp.bfloat16)
    shifted = (innovation * factor).astype(jnp.bfloat16)
    padding = jnp.zeros((7, obs_slots), jnp.bfloat16)
    obs_rows = jnp.concatenate([scaled, shifted[None, :], padding], axis=0)
    sample_slices = background_members.shape[0]
    return jnp.dot(obs_rows, obs_rows[:sample_slices].T, preferred_element_type=jnp.float32)

def inverse_root(matrix):
    size = matrix.shape[0]
    identity = jnp.eye(size, dtype=jnp.float32)
    norm_value = jnp.sqrt(jnp.sum(matrix * matrix))
    iterate = matrix / norm_value
    inverse = identity
    for iteration in range(NSTEPS):
        middle = 1.5 * identity - 0.5 * jnp.dot(inverse, iterate, precision=lax.Precision.HIGHEST)
        iterate = jnp.dot(iterate, middle, precision=lax.Precision.HIGHEST)
        inverse = jnp.dot(middle, inverse, precision=lax.Precision.HIGHEST)
    return inverse / jnp.sqrt(norm_value)

def reference(background_tensor, reading_tally, measurement_slot, reading_datum, error_precision, reading_offset):
    vertical_slices = background_tensor.shape[0]
    sample_slices = background_tensor.shape[1]

    def chosen_sample(array, vertical_slice):
        return lax.dynamic_index_in_dim(array, vertical_slice, 0, keepdims=False)

    def gram_of(vertical_slice, lateral_neighbor):
        return local_measurements(chosen_sample(background_tensor, vertical_slice), chosen_sample(measurement_slot, vertical_slice), chosen_sample(reading_tally, vertical_slice), chosen_sample(reading_datum, vertical_slice), chosen_sample(error_precision, vertical_slice), chosen_sample(reading_offset, vertical_slice), lateral_neighbor)

    def analyse(vertical_slice):
        western = (vertical_slice + vertical_slices - 1) % vertical_slices
        eastern = (vertical_slice + 1) % vertical_slices
        combined = gram_of(vertical_slice, 1) + gram_of(western, 2) + gram_of(eastern, 0)
        focal_site, anomaly_matrix = local_summary(chosen_sample(background_tensor, vertical_slice))
        identity = jnp.eye(sample_slices, dtype=jnp.float32)
        system = (sample_slices - 1) * identity + combined[:sample_slices]
        pull_vec = combined[sample_slices]
        inv_root = inverse_root(system)
        mean_weight = jnp.dot(inv_root, jnp.dot(inv_root, pull_vec, precision=lax.Precision.HIGHEST), precision=lax.Precision.HIGHEST)
        weight_matrix = (jnp.sqrt(sample_slices - 1.0) * inv_root + mean_weight[:, None]).astype(jnp.bfloat16)
        increment = jnp.dot(weight_matrix.T, anomaly_matrix, preferred_element_type=jnp.float32)
        return (focal_site[None, :] + increment).astype(jnp.bfloat16)
    return lax.map(analyse, jnp.arange(vertical_slices, dtype=jnp.int32))
```

```python
import jax
import jax.numpy as jnp
from jax import lax
from jax.sharding import PartitionSpec as P

NSTEPS = 5
F32 = jnp.float32
BF16 = jnp.bfloat16


def slot_terms(slots, tally, datum, precision, offset):
    live = (jnp.arange(slots.shape[1], dtype=jnp.int32)[None, :] < tally[:, None]).astype(F32)
    base = precision * live
    weights = [
        jnp.exp(-((offset + 0.5) ** 2)) * base,
        jnp.exp(-((offset - 0.5) ** 2)) * base,
        jnp.exp(-((1.5 - offset) ** 2)) * base,
    ]
    return jnp.stack(weights + [w * datum for w in weights], axis=1)


def split(x):
    high = lax.reduce_precision(x, 8, 7)
    return high.astype(BF16), (x - high).astype(BF16)


def regroup(terms, slots, values):
    picks = (
        jnp.arange(values, dtype=jnp.int32)[None, :, None] == slots[:, None, :]
    ).astype(BF16)
    high, low = split(terms)
    both = jnp.concatenate([high, low], axis=1)
    sums = jnp.einsum("ctm,cvm->ctv", both, picks, preferred_element_type=F32)
    return sums[:, : terms.shape[1]] + sums[:, terms.shape[1] :]


def shifted(block, axes, up):
    sizes = [lax.axis_size(axis) for axis in axes]
    count = 1
    for size in sizes:
        count *= size
    pairs = [(i, (i + 1) % count) for i in range(count)]
    if not up:
        pairs = [(target, source) for source, target in pairs]
    return lax.ppermute(block, axes, pairs)


def plain(background, tally, slots, datum, precision, offset):
    values = background.shape[2]
    sums = regroup(slot_terms(slots, tally, datum, precision, offset), slots, values)
    members = lax.all_to_all(background, "mem", split_axis=0, concat_axis=1, tiled=True)
    columns, count, _ = members.shape
    wide = members.astype(F32)
    center = jnp.sum(wide, axis=1) / count
    spread = (wide - center[:, None, :]).astype(BF16)

    def gram(which):
        weight = sums[:, which]
        scaled = (spread.astype(F32) * weight[:, None, :]).astype(BF16)
        pulls = sums[:, which + 3] - weight * center
        high, low = split(pulls)
        padding = jnp.zeros((columns, 6, values), BF16)
        rows = jnp.concatenate([scaled, high[:, None], low[:, None], padding], axis=1)
        return jnp.einsum("ekv,ejv->ekj", rows, spread, preferred_element_type=F32)

    west, own, east = gram(0), gram(1), gram(2)
    from_east = jnp.concatenate([west[1:], shifted(west[:1], ("grp", "mem"), False)], axis=0)
    from_west = jnp.concatenate([shifted(east[-1:], ("grp", "mem"), True), east[:-1]], axis=0)
    combined = own + from_east + from_west
    identity = jnp.eye(count, dtype=F32)
    system = (count - 1) * identity[None] + combined[:, :count]
    pull = combined[:, count] + combined[:, count + 1]
    norm = jnp.sqrt(jnp.sum(system * system, axis=(1, 2)))

    def product(a, b):
        return jnp.einsum("cij,cjk->cik", a, b, precision=lax.Precision.HIGH)

    iterate = system / norm[:, None, None]
    inverse = None
    for step in range(NSTEPS):
        last = step == NSTEPS - 1
        middle = 1.5 * identity[None] - 0.5 * (
            iterate if inverse is None else product(inverse, iterate)
        )
        if not last:
            iterate = product(iterate, middle)
        inverse = middle if inverse is None else product(middle, inverse)
    root = inverse / jnp.sqrt(norm)[:, None, None]
    inner = jnp.einsum("cij,cj->ci", root, pull, precision=lax.Precision.HIGHEST)
    mean = jnp.einsum("cij,cj->ci", root, inner, precision=lax.Precision.HIGHEST)
    transform = (jnp.sqrt(count - 1.0) * root + mean[:, :, None]).astype(BF16)
    increment = jnp.einsum("cjk,cjv->ckv", transform, spread, preferred_element_type=F32)
    analysis = (center[:, None, :] + increment).astype(BF16)
    return lax.all_to_all(analysis, "mem", split_axis=1, concat_axis=0, tiled=True)


def solution(mesh):
    rows = P(("grp", "mem"), None)
    in_specs = (P("grp", "mem", None), P(("grp", "mem")), rows, rows, rows, rows)
    return jax.shard_map(
        plain, mesh=mesh, in_specs=in_specs, out_specs=P("grp", "mem", None), check_vma=False
    )
```

```python
import functools

import jax
import jax.numpy as jnp
from jax import lax
from jax.experimental import pallas as pl
from jax.experimental.pallas import tpu as pltpu
from jax.sharding import PartitionSpec as P

NSTEPS = 5
F32 = jnp.float32
BF16 = jnp.bfloat16


def slot_terms(slots, tally, datum, precision, offset):
    live = (jnp.arange(slots.shape[1], dtype=jnp.int32)[None, :] < tally[:, None]).astype(F32)
    base = precision * live
    weights = [
        jnp.exp(-((offset + 0.5) ** 2)) * base,
        jnp.exp(-((offset - 0.5) ** 2)) * base,
        jnp.exp(-((1.5 - offset) ** 2)) * base,
    ]
    return jnp.stack(weights + [w * datum for w in weights], axis=1)


def split(x):
    high = lax.reduce_precision(x, 8, 7)
    return high.astype(BF16), (x - high).astype(BF16)


def regroup(terms, slots, values):
    picks = (
        jnp.arange(values, dtype=jnp.int32)[None, :, None] == slots[:, None, :]
    ).astype(BF16)
    high, low = split(terms)
    both = jnp.concatenate([high, low], axis=1)
    sums = jnp.einsum("ctm,cvm->ctv", both, picks, preferred_element_type=F32)
    return sums[:, : terms.shape[1]] + sums[:, terms.shape[1] :]


def shifted(block, axes, up):
    sizes = [lax.axis_size(axis) for axis in axes]
    count = 1
    for size in sizes:
        count *= size
    pairs = [(i, (i + 1) % count) for i in range(count)]
    if not up:
        pairs = [(target, source) for source, target in pairs]
    return lax.ppermute(block, axes, pairs)


def plain(background, tally, slots, datum, precision, offset):
    values = background.shape[2]
    sums = regroup(slot_terms(slots, tally, datum, precision, offset), slots, values)
    members = lax.all_to_all(background, "mem", split_axis=0, concat_axis=1, tiled=True)
    columns, count, _ = members.shape
    wide = members.astype(F32)
    center = jnp.sum(wide, axis=1) / count
    spread = (wide - center[:, None, :]).astype(BF16)

    def gram(which):
        weight = sums[:, which]
        scaled = (spread.astype(F32) * weight[:, None, :]).astype(BF16)
        pulls = sums[:, which + 3] - weight * center
        high, low = split(pulls)
        padding = jnp.zeros((columns, 6, values), BF16)
        rows = jnp.concatenate([scaled, high[:, None], low[:, None], padding], axis=1)
        return jnp.einsum("ekv,ejv->ekj", rows, spread, preferred_element_type=F32)

    west, own, east = gram(0), gram(1), gram(2)
    from_east = jnp.concatenate([west[1:], shifted(west[:1], ("grp", "mem"), False)], axis=0)
    from_west = jnp.concatenate([shifted(east[-1:], ("grp", "mem"), True), east[:-1]], axis=0)
    combined = own + from_east + from_west
    identity = jnp.eye(count, dtype=F32)
    system = (count - 1) * identity[None] + combined[:, :count]
    pull = combined[:, count] + combined[:, count + 1]
    norm = jnp.sqrt(jnp.sum(system * system, axis=(1, 2)))

    def product(a, b):
        return jnp.einsum("cij,cjk->cik", a, b, precision=lax.Precision.HIGH)

    iterate = system / norm[:, None, None]
    inverse = None
    for step in range(NSTEPS):
        last = step == NSTEPS - 1
        middle = 1.5 * identity[None] - 0.5 * (
            iterate if inverse is None else product(inverse, iterate)
        )
        if not last:
            iterate = product(iterate, middle)
        inverse = middle if inverse is None else product(middle, inverse)
    root = inverse / jnp.sqrt(norm)[:, None, None]
    inner = jnp.einsum("cij,cj->ci", root, pull, precision=lax.Precision.HIGHEST)
    mean = jnp.einsum("cij,cj->ci", root, inner, precision=lax.Precision.HIGHEST)
    transform = (jnp.sqrt(count - 1.0) * root + mean[:, :, None]).astype(BF16)
    increment = jnp.einsum("cjk,cjv->ckv", transform, spread, preferred_element_type=F32)
    analysis = (center[:, None, :] + increment).astype(BF16)
    return lax.all_to_all(analysis, "mem", split_axis=1, concat_axis=0, tiled=True)


NT = (((1,), (1,)), ((), ()))
NN = (((1,), (0,)), ((), ()))
PAD = 16
TILE = 256


def dot(a, b, dims=NN):
    return lax.dot_general(a, b, dims, preferred_element_type=F32)


def halves(x):
    high = x.astype(BF16)
    return high, (x - high.astype(F32)).astype(BF16)


def product(a, b):
    (ah, al), (bh, bl) = a, b
    return dot(ah, bh) + (dot(ah, bl) + dot(al, bh))


def fused_kernel(
    groups,
    ranks,
    tally_ref,
    slot_ref,
    datum_ref,
    precision_ref,
    offset_ref,
    back_ref,
    out_ref,
    got,
    spread,
    center,
    sums,
    rows,
    gram,
    from_east,
    from_west,
    stage,
    bufs,
    in_send,
    in_recv,
    out_send,
    out_recv,
    own_sem,
    side_send,
    side_recv,
):
    per, values = back_ref.shape[1], back_ref.shape[2]
    count = ranks * per
    height = count + PAD
    g, r = lax.axis_index("grp"), lax.axis_index("mem")
    total = groups * ranks
    place = g * ranks + r
    ahead = lax.rem(place + 1, total)
    behind = lax.rem(place + total - 1, total)
    east_id = (ahead // ranks, lax.rem(ahead, ranks))
    west_id = (behind // ranks, lax.rem(behind, ranks))

    barrier = pltpu.get_barrier_semaphore()

    def greet(where):
        pl.semaphore_signal(
            barrier, inc=1, device_id=where, device_id_type=pl.DeviceIdType.MESH
        )

    for i in range(1, ranks):
        greet((g, lax.rem(r + i, ranks)))
    greet(east_id)
    greet(west_id)
    pl.semaphore_wait(barrier, ranks + 1)

    def inward(c, i):
        to = lax.rem(r + i, ranks)
        return pltpu.make_async_remote_copy(
            src_ref=back_ref.at[2 * to + c],
            dst_ref=got.at[c, r],
            send_sem=in_send.at[c, i],
            recv_sem=in_recv.at[c, i],
            device_id=(g, to),
            device_id_type=pl.DeviceIdType.MESH,
        )

    def outward(c, i):
        to = lax.rem(r + i, ranks)
        return pltpu.make_async_remote_copy(
            src_ref=stage.at[c, to],
            dst_ref=out_ref.at[2 * r + c],
            send_sem=out_send.at[c, i],
            recv_sem=out_recv.at[c, i],
            device_id=(g, to),
            device_id_type=pl.DeviceIdType.MESH,
        )

    def own_in(c):
        return pltpu.make_async_copy(back_ref.at[2 * r + c], got.at[c, r], own_sem.at[c])

    def own_out(c):
        return pltpu.make_async_copy(stage.at[c, r], out_ref.at[2 * r + c], own_sem.at[2 + c])

    def sideways(k, start_row, c, landing, where):
        return pltpu.make_async_remote_copy(
            src_ref=gram.at[c, pl.ds(start_row, height)],
            dst_ref=landing,
            send_sem=side_send.at[k],
            recv_sem=side_recv.at[k],
            device_id=where,
            device_id_type=pl.DeviceIdType.MESH,
        )

    for c in range(2):
        for i in range(1, ranks):
            inward(c, i).start()
        own_in(c).start()

    lane = lax.broadcasted_iota(jnp.int32, (1, slot_ref.shape[1]), 1)
    row8 = lax.broadcasted_iota(jnp.int32, (8, slot_ref.shape[1]), 0)
    for c in range(2):
        base = jnp.where(lane < tally_ref[c], precision_ref[c : c + 1, :], 0.0)
        offset = offset_ref[c : c + 1, :]
        datum = datum_ref[c : c + 1, :]
        terms = [
            jnp.exp(-((offset + 0.5) ** 2)) * base,
            jnp.exp(-((offset - 0.5) ** 2)) * base,
            jnp.exp(-((1.5 - offset) ** 2)) * base,
        ]
        terms = terms + [t * datum for t in terms]
        stacked = jnp.zeros(row8.shape, F32)
        for k, term in enumerate(terms):
            stacked = jnp.where(row8 == k, term, stacked)
        high, low = halves(stacked)
        slots = slot_ref[c : c + 1, :]

        def collect(t, carry):
            start = pl.multiple_of(t * TILE, TILE)
            value = lax.broadcasted_iota(jnp.int32, (TILE, slots.shape[1]), 0) + start
            picks = jnp.where(value == slots, 1.0, 0.0).astype(BF16)
            sums[c, :, pl.ds(start, TILE)] = dot(high, picks, NT) + dot(low, picks, NT)
            return carry

        lax.fori_loop(0, values // TILE, collect, 0)

    row16 = lax.broadcasted_iota(jnp.int32, (PAD, TILE), 0)

    def grams(c):
        own_in(c).wait()
        for i in range(1, ranks):
            inward(c, i).wait_recv()

        def prepare(t, carry):
            start = pl.multiple_of(t * TILE, TILE)
            here = pl.ds(start, TILE)
            wide = got[c, :, :, here].reshape(count, TILE).astype(F32)
            middle = jnp.sum(wide, axis=0, keepdims=True) / count
            center[c, :, here] = middle
            away = (wide - middle).astype(BF16)
            spread[c, :, here] = away
            away = away.astype(F32)
            for k in range(3):
                weight = sums[c, k : k + 1, here]
                high, low = halves(sums[c, k + 3 : k + 4, here] - weight * middle)
                rows[k * height : k * height + count, here] = (away * weight).astype(BF16)
                pulls = jnp.where(
                    row16 == 0, high.astype(F32), jnp.where(row16 == 1, low.astype(F32), 0.0)
                )
                rows[k * height + count : (k + 1) * height, here] = pulls.astype(BF16)
            return carry

        lax.fori_loop(0, values // TILE, prepare, 0)
        for k in range(3):
            gram[c, k * height : (k + 1) * height, :] = dot(
                rows[k * height : (k + 1) * height, :], spread[c], NT
            )

    grams(0)
    westward = sideways(0, 0, 0, from_east, west_id)
    westward.start()
    grams(1)
    eastward = sideways(1, 2 * height, 1, from_west, east_id)
    eastward.start()

    square = (
        lax.broadcasted_iota(jnp.int32, (count, count), 0)
        == lax.broadcasted_iota(jnp.int32, (count, count), 1)
    )

    def middle_of(x):
        return jnp.where(square, 1.5, 0.0) - 0.5 * x

    def analyse(c, west_part, east_part):
        def combined(start, size):
            at = pl.ds(start, size)
            return gram[c, pl.ds(height + start, size), :] + west_part(at) + east_part(at)

        system = combined(0, count) + jnp.where(square, count - 1.0, 0.0)
        pulls = combined(count, 8)
        pull = pulls[0:1] + pulls[1:2]
        norm = jnp.sqrt(
            jnp.sum(jnp.sum(system * system, axis=1, keepdims=True), axis=0, keepdims=True)
        )
        first = system * (1.0 / norm)
        factor = middle_of(first)
        pair = halves(factor)
        bufs[0] = product(halves(first), pair)
        bufs[1] = factor

        def step(t, carry):
            iterate, inverse = halves(bufs[0]), halves(bufs[1])
            pair = halves(middle_of(product(inverse, iterate)))
            bufs[0] = product(iterate, pair)
            bufs[1] = product(pair, inverse)
            return carry

        lax.fori_loop(0, NSTEPS - 2, step, 0)
        iterate, inverse = halves(bufs[0]), halves(bufs[1])
        pair = halves(middle_of(product(inverse, iterate)))
        root = product(pair, inverse) * (1.0 / jnp.sqrt(norm))
        pair = halves(root)
        inner = product(halves(jnp.broadcast_to(pull, (8, count))), pair)
        mean = product(halves(inner), pair)[0:1]
        transform = (root * (count - 1.0) ** 0.5 + mean).astype(BF16)

        def apply(t, carry):
            here = pl.ds(pl.multiple_of(t * TILE, TILE), TILE)
            result = center[c, :, here] + dot(transform, spread[c, :, here])
            stage[c, :, :, here] = result.astype(BF16).reshape(ranks, per, TILE)
            return carry

        lax.fori_loop(0, values // TILE, apply, 0)
        for i in range(1, ranks):
            outward(c, i).start()
        own_out(c).start()

    westward.wait_recv()
    analyse(1, lambda at: gram[0, pl.ds(2 * height + at.start, at.size), :], lambda at: from_east[at, :])
    eastward.wait_recv()
    analyse(0, lambda at: from_west[at, :], lambda at: gram[1, at, :])
    westward.wait_send()
    eastward.wait_send()
    for c in range(2):
        own_out(c).wait()
        for i in range(1, ranks):
            inward(c, i).wait_send()
    for c in range(2):
        for i in range(1, ranks):
            outward(c, i).wait()


def fused(groups, ranks, background, tally, slots, datum, precision, offset):
    _, per, values = background.shape
    count = ranks * per
    height = count + PAD
    vmem = pl.BlockSpec(memory_space=pltpu.VMEM)
    hbm = pl.BlockSpec(memory_space=pl.ANY)
    smem = pl.BlockSpec(memory_space=pltpu.SMEM)
    dma = pltpu.SemaphoreType.DMA
    return pl.pallas_call(
        functools.partial(fused_kernel, groups, ranks),
        out_shape=jax.ShapeDtypeStruct(background.shape, background.dtype),
        in_specs=[smem, vmem, vmem, vmem, vmem, hbm],
        out_specs=hbm,
        scratch_shapes=[
            pltpu.VMEM((2, ranks, per, values), BF16),
            pltpu.VMEM((2, count, values), BF16),
            pltpu.VMEM((2, 1, values), F32),
            pltpu.VMEM((2, 8, values), F32),
            pltpu.VMEM((3 * height, values), BF16),
            pltpu.VMEM((2, 3 * height, count), F32),
            pltpu.VMEM((height, count), F32),
            pltpu.VMEM((height, count), F32),
            pltpu.VMEM((2, ranks, per, values), BF16),
            pltpu.VMEM((2, count, count), F32),
            dma((2, ranks)),
            dma((2, ranks)),
            dma((2, ranks)),
            dma((2, ranks)),
            dma((4,)),
            dma((2,)),
            dma((2,)),
        ],
        compiler_params=pltpu.CompilerParams(
            collective_id=0, has_side_effects=True, vmem_limit_bytes=48 * 1024 * 1024
        ),
    )(tally, slots, datum, precision, offset, background)


def per_device(groups, ranks, background, tally, slots, datum, precision, offset):
    columns, per, values = background.shape
    whole_tiles = per % 16 == 0 and values % TILE == 0 and (ranks * per) % 128 == 0
    if columns == 2 * ranks and whole_tiles and groups * ranks > 2:
        return fused(groups, ranks, background, tally, slots, datum, precision, offset)
    return plain(background, tally, slots, datum, precision, offset)


def solution(mesh):
    rows = P(("grp", "mem"), None)
    in_specs = (P("grp", "mem", None), P(("grp", "mem")), rows, rows, rows, rows)
    body = functools.partial(per_device, mesh.shape["grp"], mesh.shape["mem"])
    return jax.shard_map(
        body, mesh=mesh, in_specs=in_specs, out_specs=P("grp", "mem", None), check_vma=False
    )
```

```python
import functools

import jax
import jax.numpy as jnp
from jax import lax
from jax.experimental import pallas as pl
from jax.experimental.pallas import tpu as pltpu
from jax.sharding import PartitionSpec as P

NSTEPS = 5
F32 = jnp.float32
BF16 = jnp.bfloat16


def slot_terms(slots, tally, datum, precision, offset):
    live = (jnp.arange(slots.shape[1], dtype=jnp.int32)[None, :] < tally[:, None]).astype(F32)
    base = precision * live
    weights = [
        jnp.exp(-((offset + 0.5) ** 2)) * base,
        jnp.exp(-((offset - 0.5) ** 2)) * base,
        jnp.exp(-((1.5 - offset) ** 2)) * base,
    ]
    return jnp.stack(weights + [w * datum for w in weights], axis=1)


def split(x):
    high = lax.reduce_precision(x, 8, 7)
    return high.astype(BF16), (x - high).astype(BF16)


def regroup(terms, slots, values):
    picks = (
        jnp.arange(values, dtype=jnp.int32)[None, :, None] == slots[:, None, :]
    ).astype(BF16)
    high, low = split(terms)
    both = jnp.concatenate([high, low], axis=1)
    sums = jnp.einsum("ctm,cvm->ctv", both, picks, preferred_element_type=F32)
    return sums[:, : terms.shape[1]] + sums[:, terms.shape[1] :]


def shifted(block, axes, up):
    sizes = [lax.axis_size(axis) for axis in axes]
    count = 1
    for size in sizes:
        count *= size
    pairs = [(i, (i + 1) % count) for i in range(count)]
    if not up:
        pairs = [(target, source) for source, target in pairs]
    return lax.ppermute(block, axes, pairs)


def plain(background, tally, slots, datum, precision, offset):
    values = background.shape[2]
    sums = regroup(slot_terms(slots, tally, datum, precision, offset), slots, values)
    members = lax.all_to_all(background, "mem", split_axis=0, concat_axis=1, tiled=True)
    columns, count, _ = members.shape
    wide = members.astype(F32)
    center = jnp.sum(wide, axis=1) / count
    spread = (wide - center[:, None, :]).astype(BF16)

    def gram(which):
        weight = sums[:, which]
        scaled = (spread.astype(F32) * weight[:, None, :]).astype(BF16)
        pulls = sums[:, which + 3] - weight * center
        high, low = split(pulls)
        padding = jnp.zeros((columns, 6, values), BF16)
        rows = jnp.concatenate([scaled, high[:, None], low[:, None], padding], axis=1)
        return jnp.einsum("ekv,ejv->ekj", rows, spread, preferred_element_type=F32)

    west, own, east = gram(0), gram(1), gram(2)
    from_east = jnp.concatenate([west[1:], shifted(west[:1], ("grp", "mem"), False)], axis=0)
    from_west = jnp.concatenate([shifted(east[-1:], ("grp", "mem"), True), east[:-1]], axis=0)
    combined = own + from_east + from_west
    identity = jnp.eye(count, dtype=F32)
    system = (count - 1) * identity[None] + combined[:, :count]
    pull = combined[:, count] + combined[:, count + 1]
    norm = jnp.sqrt(jnp.sum(system * system, axis=(1, 2)))

    def product(a, b):
        return jnp.einsum("cij,cjk->cik", a, b, precision=lax.Precision.HIGH)

    iterate = system / norm[:, None, None]
    inverse = None
    for step in range(NSTEPS):
        last = step == NSTEPS - 1
        middle = 1.5 * identity[None] - 0.5 * (
            iterate if inverse is None else product(inverse, iterate)
        )
        if not last:
            iterate = product(iterate, middle)
        inverse = middle if inverse is None else product(middle, inverse)
    root = inverse / jnp.sqrt(norm)[:, None, None]
    inner = jnp.einsum("cij,cj->ci", root, pull, precision=lax.Precision.HIGHEST)
    mean = jnp.einsum("cij,cj->ci", root, inner, precision=lax.Precision.HIGHEST)
    transform = (jnp.sqrt(count - 1.0) * root + mean[:, :, None]).astype(BF16)
    increment = jnp.einsum("cjk,cjv->ckv", transform, spread, preferred_element_type=F32)
    analysis = (center[:, None, :] + increment).astype(BF16)
    return lax.all_to_all(analysis, "mem", split_axis=1, concat_axis=0, tiled=True)


NT = (((1,), (1,)), ((), ()))
NN = (((1,), (0,)), ((), ()))
PAD = 16
TILE = 256


def dot(a, b, dims=NN):
    return lax.dot_general(a, b, dims, preferred_element_type=F32)


def halves(x):
    high = x.astype(BF16)
    return high, (x - high.astype(F32)).astype(BF16)


def product(a, b):
    (ah, al), (bh, bl) = a, b
    return dot(ah, bh) + (dot(ah, bl) + dot(al, bh))


def fused_kernel(
    groups,
    ranks,
    tally_hbm,
    slot_hbm,
    datum_hbm,
    precision_hbm,
    offset_hbm,
    back_ref,
    out_ref,
    tally_ref,
    slot_ref,
    datum_ref,
    precision_ref,
    offset_ref,
    got,
    spread,
    center,
    sums,
    rows,
    gram,
    leaving,
    from_east,
    from_west,
    stage,
    bufs,
    in_send,
    in_recv,
    out_send,
    out_recv,
    own_sem,
    side_send,
    side_recv,
    load_sem,
):
    per, values = back_ref.shape[1], back_ref.shape[2]
    count = ranks * per
    height = count + PAD
    g, r = lax.axis_index("grp"), lax.axis_index("mem")
    total = groups * ranks
    place = g * ranks + r
    ahead = lax.rem(place + 1, total)
    behind = lax.rem(place + total - 1, total)
    east_id = (ahead // ranks, lax.rem(ahead, ranks))
    west_id = (behind // ranks, lax.rem(behind, ranks))

    loads = [
        pltpu.make_async_copy(source, target, load_sem.at[k])
        for k, (source, target) in enumerate(
            [
                (tally_hbm, tally_ref),
                (slot_hbm, slot_ref),
                (datum_hbm, datum_ref),
                (precision_hbm, precision_ref),
                (offset_hbm, offset_ref),
            ]
        )
    ]
    for load in loads:
        load.start()

    barrier = pltpu.get_barrier_semaphore()

    def greet(where):
        pl.semaphore_signal(
            barrier, inc=1, device_id=where, device_id_type=pl.DeviceIdType.MESH
        )

    for i in range(1, ranks):
        greet((g, lax.rem(r + i, ranks)))
    greet(east_id)
    greet(west_id)
    pl.semaphore_wait(barrier, ranks + 1)

    def inward(c, i):
        to = lax.rem(r + i, ranks)
        return pltpu.make_async_remote_copy(
            src_ref=back_ref.at[2 * to + c],
            dst_ref=got.at[c, r],
            send_sem=in_send.at[c, i],
            recv_sem=in_recv.at[c, i],
            device_id=(g, to),
            device_id_type=pl.DeviceIdType.MESH,
        )

    def outward(c, i):
        to = lax.rem(r + i, ranks)
        return pltpu.make_async_remote_copy(
            src_ref=stage.at[c, to],
            dst_ref=out_ref.at[2 * r + c],
            send_sem=out_send.at[c, i],
            recv_sem=out_recv.at[c, i],
            device_id=(g, to),
            device_id_type=pl.DeviceIdType.MESH,
        )

    def own_in(c):
        return pltpu.make_async_copy(back_ref.at[2 * r + c], got.at[c, r], own_sem.at[c])

    def own_out(c):
        return pltpu.make_async_copy(stage.at[c, r], out_ref.at[2 * r + c], own_sem.at[2 + c])

    def sideways(k, landing, where):
        return pltpu.make_async_remote_copy(
            src_ref=leaving.at[k],
            dst_ref=landing,
            send_sem=side_send.at[k],
            recv_sem=side_recv.at[k],
            device_id=where,
            device_id_type=pl.DeviceIdType.MESH,
        )

    order = list(range(1, ranks))
    early = (len(order) + 1) // 2
    for i in order:
        inward(0, i).start()
    own_in(0).start()
    for i in order[:early]:
        inward(1, i).start()
    own_in(1).start()
    for load in loads:
        load.wait()

    lane = lax.broadcasted_iota(jnp.int32, (1, slot_ref.shape[1]), 1)
    row8 = lax.broadcasted_iota(jnp.int32, (8, slot_ref.shape[1]), 0)
    for c in range(2):
        base = jnp.where(lane < tally_ref[c], precision_ref[c : c + 1, :], 0.0)
        offset = offset_ref[c : c + 1, :]
        datum = datum_ref[c : c + 1, :]
        terms = [
            jnp.exp(-((offset + 0.5) ** 2)) * base,
            jnp.exp(-((offset - 0.5) ** 2)) * base,
            jnp.exp(-((1.5 - offset) ** 2)) * base,
        ]
        terms = terms + [t * datum for t in terms]
        stacked = jnp.zeros(row8.shape, F32)
        for k, term in enumerate(terms):
            stacked = jnp.where(row8 == k, term, stacked)
        high, low = halves(stacked)
        slots = slot_ref[c : c + 1, :]

        def collect(t, carry):
            start = pl.multiple_of(t * TILE, TILE)
            value = lax.broadcasted_iota(jnp.int32, (TILE, slots.shape[1]), 0) + start
            picks = jnp.where(value == slots, 1.0, 0.0).astype(BF16)
            sums[c, :, pl.ds(start, TILE)] = dot(high, picks, NT) + dot(low, picks, NT)
            return carry

        lax.fori_loop(0, values // TILE, collect, 0)

    row16 = lax.broadcasted_iota(jnp.int32, (PAD, TILE), 0)

    def grams(c):
        own_in(c).wait()
        for i in range(1, ranks):
            inward(c, i).wait_recv()

        def prepare(t, carry):
            start = pl.multiple_of(t * TILE, TILE)
            here = pl.ds(start, TILE)
            wide = got[c, :, :, here].reshape(count, TILE).astype(F32)
            middle = jnp.sum(wide, axis=0, keepdims=True) / count
            center[c, :, here] = middle
            away = (wide - middle).astype(BF16)
            spread[c, :, here] = away
            away = away.astype(F32)
            for k in range(3):
                weight = sums[c, k : k + 1, here]
                high, low = halves(sums[c, k + 3 : k + 4, here] - weight * middle)
                rows[k * height : k * height + count, here] = (away * weight).astype(BF16)
                pulls = jnp.where(
                    row16 == 0, high.astype(F32), jnp.where(row16 == 1, low.astype(F32), 0.0)
                )
                rows[k * height + count : (k + 1) * height, here] = pulls.astype(BF16)
            return carry

        lax.fori_loop(0, values // TILE, prepare, 0)
        for k in range(3):
            gram[c, k * height : (k + 1) * height, :] = dot(
                rows[k * height : (k + 1) * height, :], spread[c], NT
            )

    grams(0)
    leaving[0] = gram[0, 0:height, :].astype(BF16)
    westward = sideways(0, from_east, west_id)
    westward.start()
    for i in order[early:]:
        inward(1, i).start()
    grams(1)
    leaving[1] = gram[1, 2 * height : 3 * height, :].astype(BF16)
    eastward = sideways(1, from_west, east_id)
    eastward.start()

    square = (
        lax.broadcasted_iota(jnp.int32, (count, count), 0)
        == lax.broadcasted_iota(jnp.int32, (count, count), 1)
    )

    def middle_of(x):
        return jnp.where(square, 1.5, 0.0) - 0.5 * x

    def analyse(c, west_part, east_part):
        def combined(start, size):
            at = pl.ds(start, size)
            return gram[c, pl.ds(height + start, size), :] + west_part(at) + east_part(at)

        system = combined(0, count) + jnp.where(square, count - 1.0, 0.0)
        pulls = combined(count, PAD)
        pull = pulls[0:1] + pulls[1:2]
        norm = jnp.sqrt(
            jnp.sum(jnp.sum(system * system, axis=1, keepdims=True), axis=0, keepdims=True)
        )
        first = system * (1.0 / norm)
        factor = middle_of(first)
        pair = halves(factor)
        bufs[0] = product(halves(first), pair)
        bufs[1] = factor

        def step(t, carry):
            iterate, inverse = halves(bufs[0]), halves(bufs[1])
            pair = halves(middle_of(product(inverse, iterate)))
            bufs[0] = product(iterate, pair)
            bufs[1] = product(pair, inverse)
            return carry

        lax.fori_loop(0, NSTEPS - 2, step, 0)
        iterate, inverse = halves(bufs[0]), halves(bufs[1])
        pair = halves(middle_of(product(inverse, iterate)))
        root = product(pair, inverse) * (1.0 / jnp.sqrt(norm))
        pair = halves(root)
        inner = product(halves(jnp.broadcast_to(pull, (8, count))), pair)
        mean = product(halves(inner), pair)[0:1]
        transform = (root * (count - 1.0) ** 0.5 + mean).astype(BF16)

        def apply(t, carry):
            here = pl.ds(pl.multiple_of(t * TILE, TILE), TILE)
            result = center[c, :, here] + dot(transform, spread[c, :, here])
            stage[c, :, :, here] = result.astype(BF16).reshape(ranks, per, TILE)
            return carry

        lax.fori_loop(0, values // TILE, apply, 0)
        for i in range(1, ranks):
            outward(c, i).start()
        own_out(c).start()

    westward.wait_recv()
    analyse(1, lambda at: gram[0, pl.ds(2 * height + at.start, at.size), :], lambda at: from_east[at, :].astype(F32))
    eastward.wait_recv()
    analyse(0, lambda at: from_west[at, :].astype(F32), lambda at: gram[1, at, :])
    westward.wait_send()
    eastward.wait_send()
    for c in range(2):
        own_out(c).wait()
        for i in range(1, ranks):
            inward(c, i).wait_send()
    for c in range(2):
        for i in range(1, ranks):
            outward(c, i).wait()


def fused(groups, ranks, background, tally, slots, datum, precision, offset):
    _, per, values = background.shape
    count = ranks * per
    height = count + PAD
    hbm = pl.BlockSpec(memory_space=pl.ANY)
    observed = pltpu.VMEM(slots.shape, F32)
    dma = pltpu.SemaphoreType.DMA
    return pl.pallas_call(
        functools.partial(fused_kernel, groups, ranks),
        out_shape=jax.ShapeDtypeStruct(background.shape, background.dtype),
        in_specs=[hbm] * 6,
        out_specs=hbm,
        scratch_shapes=[
            pltpu.SMEM(tally.shape, jnp.int32),
            pltpu.VMEM(slots.shape, jnp.int32),
            observed,
            observed,
            observed,
            pltpu.VMEM((2, ranks, per, values), BF16),
            pltpu.VMEM((2, count, values), BF16),
            pltpu.VMEM((2, 1, values), F32),
            pltpu.VMEM((2, 8, values), F32),
            pltpu.VMEM((3 * height, values), BF16),
            pltpu.VMEM((2, 3 * height, count), F32),
            pltpu.VMEM((2, height, count), BF16),
            pltpu.VMEM((height, count), BF16),
            pltpu.VMEM((height, count), BF16),
            pltpu.VMEM((2, ranks, per, values), BF16),
            pltpu.VMEM((2, count, count), F32),
            dma((2, ranks)),
            dma((2, ranks)),
            dma((2, ranks)),
            dma((2, ranks)),
            dma((4,)),
            dma((2,)),
            dma((2,)),
            dma((5,)),
        ],
        compiler_params=pltpu.CompilerParams(
            collective_id=0, has_side_effects=True, vmem_limit_bytes=67043328
        ),
    )(tally, slots, datum, precision, offset, background)


def per_device(groups, ranks, background, tally, slots, datum, precision, offset):
    columns, per, values = background.shape
    whole_tiles = per % 16 == 0 and values % TILE == 0 and (ranks * per) % 128 == 0
    if columns == 2 * ranks and whole_tiles and groups * ranks > 2:
        return fused(groups, ranks, background, tally, slots, datum, precision, offset)
    return plain(background, tally, slots, datum, precision, offset)


def solution(mesh):
    rows = P(("grp", "mem"), None)
    in_specs = (P("grp", "mem", None), P(("grp", "mem")), rows, rows, rows, rows)
    body = functools.partial(per_device, mesh.shape["grp"], mesh.shape["mem"])
    return jax.shard_map(
        body, mesh=mesh, in_specs=in_specs, out_specs=P("grp", "mem", None), check_vma=False
    )
```

```python
import functools

import jax
import jax.numpy as jnp
from jax import lax
from jax.experimental import pallas as pl
from jax.experimental.pallas import tpu as pltpu
from jax.sharding import PartitionSpec as P

NSTEPS = 5
F32 = jnp.float32
BF16 = jnp.bfloat16


def slot_terms(slots, tally, datum, precision, offset):
    live = (jnp.arange(slots.shape[1], dtype=jnp.int32)[None, :] < tally[:, None]).astype(F32)
    base = precision * live
    weights = [
        jnp.exp(-((offset + 0.5) ** 2)) * base,
        jnp.exp(-((offset - 0.5) ** 2)) * base,
        jnp.exp(-((1.5 - offset) ** 2)) * base,
    ]
    return jnp.stack(weights + [w * datum for w in weights], axis=1)


def split(x):
    high = lax.reduce_precision(x, 8, 7)
    return high.astype(BF16), (x - high).astype(BF16)


def regroup(terms, slots, values):
    picks = (
        jnp.arange(values, dtype=jnp.int32)[None, :, None] == slots[:, None, :]
    ).astype(BF16)
    high, low = split(terms)
    both = jnp.concatenate([high, low], axis=1)
    sums = jnp.einsum("ctm,cvm->ctv", both, picks, preferred_element_type=F32)
    return sums[:, : terms.shape[1]] + sums[:, terms.shape[1] :]


def shifted(block, axes, up):
    sizes = [lax.axis_size(axis) for axis in axes]
    count = 1
    for size in sizes:
        count *= size
    pairs = [(i, (i + 1) % count) for i in range(count)]
    if not up:
        pairs = [(target, source) for source, target in pairs]
    return lax.ppermute(block, axes, pairs)


def plain(background, tally, slots, datum, precision, offset):
    values = background.shape[2]
    sums = regroup(slot_terms(slots, tally, datum, precision, offset), slots, values)
    members = lax.all_to_all(background, "mem", split_axis=0, concat_axis=1, tiled=True)
    columns, count, _ = members.shape
    wide = members.astype(F32)
    center = jnp.sum(wide, axis=1) / count
    spread = (wide - center[:, None, :]).astype(BF16)

    def gram(which):
        weight = sums[:, which]
        scaled = (spread.astype(F32) * weight[:, None, :]).astype(BF16)
        pulls = sums[:, which + 3] - weight * center
        high, low = split(pulls)
        padding = jnp.zeros((columns, 6, values), BF16)
        rows = jnp.concatenate([scaled, high[:, None], low[:, None], padding], axis=1)
        return jnp.einsum("ekv,ejv->ekj", rows, spread, preferred_element_type=F32)

    west, own, east = gram(0), gram(1), gram(2)
    from_east = jnp.concatenate([west[1:], shifted(west[:1], ("grp", "mem"), False)], axis=0)
    from_west = jnp.concatenate([shifted(east[-1:], ("grp", "mem"), True), east[:-1]], axis=0)
    combined = own + from_east + from_west
    identity = jnp.eye(count, dtype=F32)
    system = (count - 1) * identity[None] + combined[:, :count]
    pull = combined[:, count] + combined[:, count + 1]
    norm = jnp.sqrt(jnp.sum(system * system, axis=(1, 2)))

    def product(a, b):
        return jnp.einsum("cij,cjk->cik", a, b, precision=lax.Precision.HIGH)

    iterate = system / norm[:, None, None]
    inverse = None
    for step in range(NSTEPS):
        last = step == NSTEPS - 1
        middle = 1.5 * identity[None] - 0.5 * (
            iterate if inverse is None else product(inverse, iterate)
        )
        if not last:
            iterate = product(iterate, middle)
        inverse = middle if inverse is None else product(middle, inverse)
    root = inverse / jnp.sqrt(norm)[:, None, None]
    inner = jnp.einsum("cij,cj->ci", root, pull, precision=lax.Precision.HIGHEST)
    mean = jnp.einsum("cij,cj->ci", root, inner, precision=lax.Precision.HIGHEST)
    transform = (jnp.sqrt(count - 1.0) * root + mean[:, :, None]).astype(BF16)
    increment = jnp.einsum("cjk,cjv->ckv", transform, spread, preferred_element_type=F32)
    analysis = (center[:, None, :] + increment).astype(BF16)
    return lax.all_to_all(analysis, "mem", split_axis=1, concat_axis=0, tiled=True)


NT = (((1,), (1,)), ((), ()))
NN = (((1,), (0,)), ((), ()))
PAD = 16
TILE = 256


def dot(a, b, dims=NN):
    return lax.dot_general(a, b, dims, preferred_element_type=F32)


def halves(x):
    high = x.astype(BF16)
    return high, (x - high.astype(F32)).astype(BF16)


def product(a, b):
    (ah, al), (bh, bl) = a, b
    return dot(ah, bh) + (dot(ah, bl) + dot(al, bh))


def fused_kernel(
    groups,
    ranks,
    tally_hbm,
    slot_hbm,
    datum_hbm,
    precision_hbm,
    offset_hbm,
    back_ref,
    out_ref,
    tally_ref,
    slot_ref,
    datum_ref,
    precision_ref,
    offset_ref,
    got,
    spread,
    center,
    sums,
    rows,
    gram,
    leaving,
    landing,
    mine,
    stage,
    bufs,
    in_send,
    in_recv,
    out_send,
    out_recv,
    own_sem,
    side_send,
    side_recv,
    load_sem,
    sum_send,
    sum_recv,
    sum_own,
):
    per, values = back_ref.shape[1], back_ref.shape[2]
    count = ranks * per
    height = count + PAD
    g, r = lax.axis_index("grp"), lax.axis_index("mem")
    total = groups * ranks
    place = g * ranks + r
    ahead = lax.rem(place + 1, total)
    behind = lax.rem(place + total - 1, total)
    east_id = (ahead // ranks, lax.rem(ahead, ranks))
    west_id = (behind // ranks, lax.rem(behind, ranks))

    loads = [
        pltpu.make_async_copy(source, target, load_sem.at[k])
        for k, (source, target) in enumerate(
            [
                (tally_hbm, tally_ref),
                (slot_hbm, slot_ref),
                (datum_hbm, datum_ref),
                (precision_hbm, precision_ref),
                (offset_hbm, offset_ref),
            ]
        )
    ]
    for load in loads:
        load.start()

    half = ranks // 2
    inner = jnp.logical_and(r > 0, r < ranks - 1)

    def column(where, c):
        if c == 0:
            return half + where
        return jnp.where(where < half, where, ranks + where)

    def seat(col):
        middle = jnp.logical_and(col >= half, col < half + ranks)
        outer = jnp.where(col < half, col, col - ranks)
        return jnp.where(middle, col - half, outer), jnp.where(middle, 0, 1)

    side = (r // half) * half

    def partner(i):
        if i < half:
            return half - side + lax.rem(r + i, half)
        return side + lax.rem(r + i - half, half)

    barrier = pltpu.get_barrier_semaphore()

    def greet(where):
        pl.semaphore_signal(
            barrier, inc=1, device_id=where, device_id_type=pl.DeviceIdType.MESH
        )

    for i in range(1, ranks):
        greet((g, lax.rem(r + i, ranks)))
    greet(east_id)
    greet(west_id)
    pl.semaphore_wait(barrier, ranks + 1)

    def inward(c, i):
        to = partner(i)
        return pltpu.make_async_remote_copy(
            src_ref=back_ref.at[column(to, c)],
            dst_ref=got.at[c, r],
            send_sem=in_send.at[c, i],
            recv_sem=in_recv.at[c, i],
            device_id=(g, to),
            device_id_type=pl.DeviceIdType.MESH,
        )

    def outward(c, i):
        to = partner(i)
        return pltpu.make_async_remote_copy(
            src_ref=stage.at[c, to],
            dst_ref=out_ref.at[column(r, c)],
            send_sem=out_send.at[c, i],
            recv_sem=out_recv.at[c, i],
            device_id=(g, to),
            device_id_type=pl.DeviceIdType.MESH,
        )

    def own_in(c):
        return pltpu.make_async_copy(back_ref.at[column(r, c)], got.at[c, r], own_sem.at[c])

    def own_out(c):
        return pltpu.make_async_copy(stage.at[c, r], out_ref.at[column(r, c)], own_sem.at[2 + c])

    def sideways(c, way):
        edge, back = (0, -1) if way == 0 else (ranks - 1, 1)
        turn = half if way == 0 else half - 1
        far = half - 1 if way == 0 else half
        if c == 0:
            group = g
            to = jnp.where(r == edge, far, r + back)
            phase = jnp.where(r == edge, 1, 0)
        else:
            group = jnp.where(r == edge, lax.rem(g + back + groups, groups), g)
            to = jnp.where(
                r == edge,
                ranks - 1 - edge,
                jnp.where(r == turn, ranks - 1 if way == 0 else 0, r + back),
            )
            phase = jnp.where(r == turn, 0, 1)
        return pltpu.make_async_remote_copy(
            src_ref=leaving.at[c, way],
            dst_ref=landing.at[way, phase],
            send_sem=side_send.at[c, way],
            recv_sem=side_recv.at[way, phase],
            device_id=(group, to),
            device_id_type=pl.DeviceIdType.MESH,
        )

    def arrival(c, way):
        return pltpu.make_async_remote_copy(
            src_ref=leaving.at[c, way],
            dst_ref=landing.at[way, c],
            send_sem=side_send.at[c, way],
            recv_sem=side_recv.at[way, c],
            device_id=(g, lax.rem(r + 1, ranks)),
            device_id_type=pl.DeviceIdType.MESH,
        )

    def sum_out(c, to, phase):
        return pltpu.make_async_remote_copy(
            src_ref=mine.at[c],
            dst_ref=sums.at[phase],
            send_sem=sum_send.at[c],
            recv_sem=sum_recv.at[phase],
            device_id=(g, to),
            device_id_type=pl.DeviceIdType.MESH,
        )

    def sum_stay(c, phase):
        return pltpu.make_async_copy(mine.at[c], sums.at[phase], sum_own.at[c])

    order = [i for i in range(ranks) if i != half]
    early, first = half//2, half//2
    for i in order:
        inward(0, i).start()
    own_in(0).start()
    own_in(1).start()
    for load in loads:
        load.wait()

    lane = lax.broadcasted_iota(jnp.int32, (1, slot_ref.shape[1]), 1)
    row8 = lax.broadcasted_iota(jnp.int32, (8, slot_ref.shape[1]), 0)
    for c in range(2):
        base = jnp.where(lane < tally_ref[c], precision_ref[c : c + 1, :], 0.0)
        offset = offset_ref[c : c + 1, :]
        datum = datum_ref[c : c + 1, :]
        terms = [
            jnp.exp(-((offset + 0.5) ** 2)) * base,
            jnp.exp(-((offset - 0.5) ** 2)) * base,
            jnp.exp(-((1.5 - offset) ** 2)) * base,
        ]
        terms = terms + [t * datum for t in terms]
        stacked = jnp.zeros(row8.shape, F32)
        for k, term in enumerate(terms):
            stacked = jnp.where(row8 == k, term, stacked)
        high, low = halves(stacked)
        slots = slot_ref[c : c + 1, :]

        def collect(t, carry):
            start = pl.multiple_of(t * TILE, TILE)
            value = lax.broadcasted_iota(jnp.int32, (TILE, slots.shape[1]), 0) + start
            picks = jnp.where(value == slots, 1.0, 0.0).astype(BF16)
            mine[c, :, pl.ds(start, TILE)] = dot(high, picks, NT) + dot(low, picks, NT)
            return carry

        lax.fori_loop(0, values // TILE, collect, 0)
        to, phase = seat(2 * r + c)

        @pl.when(to != r)
        def _():
            sum_out(c, to, phase).start()

        @pl.when(to == r)
        def _():
            sum_stay(c, phase).start()

    for i in order[:early]:
        inward(1, i).start()

    row16 = lax.broadcasted_iota(jnp.int32, (PAD, TILE), 0)

    def grams(c):
        owner = column(r, c) // 2
        mate = lax.rem(column(r, c), 2)

        @pl.when(owner != r)
        def _():
            sum_out(0, lax.rem(r + 1, ranks), c).wait_recv()

        @pl.when(owner == r)
        def _():
            pltpu.make_async_copy(mine.at[mate], sums.at[c], sum_own.at[mate]).wait()

        own_in(c).wait()
        for i in order:
            inward(c, i).wait_recv()

        def prepare(t, carry):
            start = pl.multiple_of(t * TILE, TILE)
            here = pl.ds(start, TILE)
            wide = got[c, :, :, here].reshape(count, TILE).astype(F32)
            middle = jnp.sum(wide, axis=0, keepdims=True) / count
            center[c, :, here] = middle
            away = (wide - middle).astype(BF16)
            spread[c, :, here] = away
            away = away.astype(F32)
            for k in range(3):
                weight = sums[c, k : k + 1, here]
                high, low = halves(sums[c, k + 3 : k + 4, here] - weight * middle)
                rows[k * height : k * height + count, here] = (away * weight).astype(BF16)
                pulls = jnp.where(
                    row16 == 0, high.astype(F32), jnp.where(row16 == 1, low.astype(F32), 0.0)
                )
                rows[k * height + count : (k + 1) * height, here] = pulls.astype(BF16)
            return carry

        lax.fori_loop(0, values // TILE, prepare, 0)

        def gram_of(k):
            return dot(rows[k * height : (k + 1) * height, :], spread[c], NT)

        for way, k in ((0, 0), (1, 2)):
            leaving[c, way] = gram_of(k).astype(BF16)
            sideways(c, way).start()
        gram[c] = gram_of(1)

    square = (
        lax.broadcasted_iota(jnp.int32, (count, count), 0)
        == lax.broadcasted_iota(jnp.int32, (count, count), 1)
    )

    def middle_of(x):
        return jnp.where(square, 1.5, 0.0) - 0.5 * x

    def analyse(c):
        for way in range(2):
            arrival(c, way).wait_recv()

        def combined(start, size):
            at = pl.ds(start, size)
            sides = landing[0, c, at, :].astype(F32) + landing[1, c, at, :].astype(F32)
            return gram[c, at, :] + sides

        system = combined(0, count) + jnp.where(square, count - 1.0, 0.0)
        pulls = combined(count, PAD)
        pull = pulls[0:1] + pulls[1:2]
        norm = jnp.sqrt(
            jnp.sum(jnp.sum(system * system, axis=1, keepdims=True), axis=0, keepdims=True)
        )
        first = system * (1.0 / norm)
        factor = middle_of(first)
        pair = halves(factor)
        bufs[0] = product(halves(first), pair)
        bufs[1] = factor

        def step(t, carry):
            iterate, inverse = halves(bufs[0]), halves(bufs[1])
            pair = halves(middle_of(product(inverse, iterate)))
            bufs[0] = product(iterate, pair)
            bufs[1] = product(pair, inverse)
            return carry

        lax.fori_loop(0, NSTEPS - 2, step, 0)
        iterate, inverse = halves(bufs[0]), halves(bufs[1])
        pair = halves(middle_of(product(inverse, iterate)))
        root = product(pair, inverse) * (1.0 / jnp.sqrt(norm))
        pair = halves(root)
        inner = product(halves(jnp.broadcast_to(pull, (8, count))), pair)
        mean = product(halves(inner), pair)[0:1]
        transform = (root * (count - 1.0) ** 0.5 + mean).astype(BF16)

        def apply(t, carry):
            here = pl.ds(pl.multiple_of(t * TILE, TILE), TILE)
            result = center[c, :, here] + dot(transform, spread[c, :, here])
            stage[c, :, :, here] = result.astype(BF16).reshape(ranks, per, TILE)
            return carry

        lax.fori_loop(0, values // TILE, apply, 0)
        own_out(c).start()

    def release(c, which):
        for i in which:
            outward(c, i).start()

    grams(0)
    for i in order[early:]:
        inward(1, i).start()

    @pl.when(inner)
    def _():
        analyse(0)
        release(0, order[:first])

    grams(1)

    @pl.when(inner)
    def _():
        release(0, order[first:])

    @pl.when(jnp.logical_not(inner))
    def _():
        analyse(0)
        release(0, order)

    analyse(1)
    release(1, order)
    for c in range(2):
        to, phase = seat(2 * r + c)

        @pl.when(to != r)
        def _():
            sum_out(c, to, phase).wait_send()

        for way in range(2):
            sideways(c, way).wait_send()
    for c in range(2):
        own_out(c).wait()
        for i in order:
            inward(c, i).wait_send()
    for c in range(2):
        for i in order:
            outward(c, i).wait()


def fused(groups, ranks, background, tally, slots, datum, precision, offset):
    _, per, values = background.shape
    count = ranks * per
    height = count + PAD
    hbm = pl.BlockSpec(memory_space=pl.ANY)
    observed = pltpu.VMEM(slots.shape, F32)
    dma = pltpu.SemaphoreType.DMA
    return pl.pallas_call(
        functools.partial(fused_kernel, groups, ranks),
        out_shape=jax.ShapeDtypeStruct(background.shape, background.dtype),
        in_specs=[hbm] * 6,
        out_specs=hbm,
        scratch_shapes=[
            pltpu.SMEM(tally.shape, jnp.int32),
            pltpu.VMEM(slots.shape, jnp.int32),
            observed,
            observed,
            observed,
            pltpu.VMEM((2, ranks, per, values), BF16),
            pltpu.VMEM((2, count, values), BF16),
            pltpu.VMEM((2, 1, values), F32),
            pltpu.VMEM((2, 8, values), F32),
            pltpu.VMEM((3 * height, values), BF16),
            pltpu.VMEM((2, height, count), F32),
            pltpu.VMEM((2, 2, height, count), BF16),
            pltpu.VMEM((2, 2, height, count), BF16),
            pltpu.VMEM((2, 8, values), F32),
            pltpu.VMEM((2, ranks, per, values), BF16),
            pltpu.VMEM((2, count, count), F32),
            dma((2, ranks)),
            dma((2, ranks)),
            dma((2, ranks)),
            dma((2, ranks)),
            dma((4,)),
            dma((2, 2)),
            dma((2, 2)),
            dma((5,)),
            dma((2,)),
            dma((2,)),
            dma((2,)),
        ],
        compiler_params=pltpu.CompilerParams(
            collective_id=0, has_side_effects=True, vmem_limit_bytes=67043328
        ),
    )(tally, slots, datum, precision, offset, background)


def per_device(groups, ranks, background, tally, slots, datum, precision, offset):
    columns, per, values = background.shape
    whole_tiles = per % 16 == 0 and values % TILE == 0 and (ranks * per) % 128 == 0
    if columns == 2 * ranks and whole_tiles and ranks % 2 == 0 and ranks > 2:
        return fused(groups, ranks, background, tally, slots, datum, precision, offset)
    return plain(background, tally, slots, datum, precision, offset)


def solution(mesh):
    rows = P(("grp", "mem"), None)
    in_specs = (P("grp", "mem", None), P(("grp", "mem")), rows, rows, rows, rows)
    body = functools.partial(per_device, mesh.shape["grp"], mesh.shape["mem"])
    return jax.shard_map(
        body, mesh=mesh, in_specs=in_specs, out_specs=P("grp", "mem", None), check_vma=False
    )
```
